32 devices in a mesh: grp: 2 (over x), tok: 8 (over z, y), wid: 2 (over core).
Axes of the slice: x: 2, y: 2, z: 4, core: 2. Of those that a mesh axis runs over, the one named last changes fastest.
Arguments:
- inputs: bfloat16 [128, 8192], P(('grp', 'wid'), 'tok'), may hold values from -6 to 6
- parent_gate: bfloat16 [8192, 28672], P('tok', ('grp', 'wid')), may hold values from -0.0625 to 0.0625
- parent_up: bfloat16 [8192, 28672], P('tok', ('grp', 'wid')), may hold values from -0.0625 to 0.0625
- parent_down: bfloat16 [28672, 8192], P(('grp', 'wid'), 'tok'), may hold values from -0.03125 to 0.03125
- first_gate: bfloat16 [8192, 7168], P('tok', ('grp', 'wid')), may hold values from -0.0625 to 0.0625
- first_up: bfloat16 [8192, 7168], P('tok', ('grp', 'wid')), may hold values from -0.0625 to 0.0625
- first_down: bfloat16 [7168, 8192], P(('grp', 'wid'), 'tok'), may hold values from -0.0625 to 0.0625
- second_gate: bfloat16 [8192, 5632], P('tok', ('grp', 'wid')), may hold values from -0.0625 to 0.0625
- second_up: bfloat16 [8192, 5632], P('tok', ('grp', 'wid')), may hold values from -0.0625 to 0.0625
- second_down: bfloat16 [5632, 8192], P(('grp', 'wid'), 'tok'), may hold values from -0.078125 to 0.078125
Outputs:
- target: bfloat16 [128, 8192], P(('grp', 'wid'), 'tok')
- first_error: bfloat16 [128, 8192], P(('grp', 'wid'), 'tok')
- second_error: bfloat16 [128, 8192], P(('grp', 'wid'), 'tok')
- first_grad_gate: bfloat16 [8192, 7168], P('tok', ('grp', 'wid'))
- first_grad_up: bfloat16 [8192, 7168], P('tok', ('grp', 'wid'))
- first_grad_down: bfloat16 [7168, 8192], P(('grp', 'wid'), 'tok')
- second_grad_gate: bfloat16 [8192, 5632], P('tok', ('grp', 'wid'))
- second_grad_up: bfloat16 [8192, 5632], P('tok', ('grp', 'wid'))
- second_grad_down: bfloat16 [5632, 8192], P(('grp', 'wid'), 'tok')
The draws below stay inside these ranges and needn't reach their ends.
All inputs are finite; a program needn't handle non-finite values.
Results may differ from the reference program's by a relative error of at most 0.009.
Values may be sent and summed in bfloat16 or wider, within the bound.
A program may use at most 192 MiB of HBM per device.

```python
import jax
import jax.numpy as jnp
from jax import lax

D = 8192
FF = 28672
HA = 7168
HB = 5632
TOKENS = 128


def level_of(rng, extent, shards, low, top_value):
    factor_of = 1.0
    for axis_at, shards_of in shards:
        steps = jax.random.uniform(jax.random.fold_in(jax.random.fold_in(rng, 6), axis_at), (shards_of,), jnp.float32, low / len(shards), top_value / len(shards))
        factor_of = factor_of * jnp.repeat(jnp.exp(steps), extent[axis_at] // shards_of).reshape((-1,) + (1,) * (len(extent) - 1 - axis_at))
    return factor_of


def normal_values(own_key, extent, width, limit, pieces=(), kind=jnp.bfloat16):
    drawn = jax.random.normal(own_key, extent, jnp.float32) * width
    if len(pieces) > 0:
        drawn = level_of(own_key, extent, pieces, -0.22, 0.18) * drawn
    return jnp.clip(drawn, min=-limit, max=limit).astype(kind)


def setup_inputs(seed: int = 0) -> dict:
    arg_keys = jax.random.split(jax.random.key(seed), 11)
    inputs = normal_values(arg_keys[0], (TOKENS, D), 1.0, 6.0, ((0, 4), (1, 8)))
    parent_gate = normal_values(arg_keys[1], (D, FF), D ** -0.5, 0.0625, ((0, 8), (1, 4)))
    parent_up = normal_values(arg_keys[2], (D, FF), D ** -0.5, 0.0625, ((0, 8), (1, 4)))
    parent_down = normal_values(arg_keys[3], (FF, D), FF ** -0.5, 0.03125, ((0, 4), (1, 8)))
    first_gate = normal_values(arg_keys[4], (D, HA), D ** -0.5, 0.0625, ((0, 8), (1, 4)))
    first_up = normal_values(arg_keys[5], (D, HA), D ** -0.5, 0.0625, ((0, 8), (1, 4)))
    first_down = normal_values(arg_keys[6], (HA, D), HA ** -0.5, 0.0625, ((0, 4), (1, 8)))
    second_gate = normal_values(arg_keys[7], (D, HB), D ** -0.5, 0.0625, ((0, 8), (1, 4)))
    second_up = normal_values(arg_keys[8], (D, HB), D ** -0.5, 0.0625, ((0, 8), (1, 4)))
    second_down = normal_values(arg_keys[9], (HB, D), HB ** -0.5, 0.078125, ((0, 4), (1, 8)))
    return dict(inputs=inputs, parent_gate=parent_gate, parent_up=parent_up, parent_down=parent_down, first_gate=first_gate, first_up=first_up, first_down=first_down, second_gate=second_gate, second_up=second_up, second_down=second_down)


def matmul(left, right):
    return jnp.dot(left, right, preferred_element_type=jnp.float32)


def inner_rows(left, right):
    return lax.dot_general(left, right, (((0,), (0,)), ((), ())), preferred_element_type=jnp.float32)


def outer_cols(left, right):
    return lax.dot_general(left, right, (((1,), (1,)), ((), ())), preferred_element_type=jnp.float32)


def candidate_pass(inputs, target, gate_w, up_w, down_w):
    pre_gate = matmul(inputs, gate_w)
    pre_up = matmul(inputs, up_w)
    hidden = (jax.nn.silu(pre_gate) * pre_up).astype(jnp.bfloat16)
    output_full = matmul(hidden, down_w)
    error_vals = (output_full - target.astype(jnp.float32)).astype(jnp.bfloat16)
    grad_down = inner_rows(hidden, error_vals).astype(jnp.bfloat16)
    back_grad = outer_cols(error_vals, down_w)
    sigmoid_gate = jax.nn.sigmoid(pre_gate)
    grad_pre_gate = (back_grad * pre_up * sigmoid_gate * (1.0 + pre_gate * (1.0 - sigmoid_gate))).astype(jnp.bfloat16)
    grad_pre_up = (back_grad * pre_gate * sigmoid_gate).astype(jnp.bfloat16)
    grad_gate = inner_rows(inputs, grad_pre_gate).astype(jnp.bfloat16)
    grad_up = inner_rows(inputs, grad_pre_up).astype(jnp.bfloat16)
    return error_vals, grad_gate, grad_up, grad_down


def reference(inputs, parent_gate, parent_up, parent_down, first_gate, first_up, first_down, second_gate, second_up, second_down):
    parent_pre_gate = matmul(inputs, parent_gate)
    parent_pre_up = matmul(inputs, parent_up)
    parent_hidden = (jax.nn.silu(parent_pre_gate) * parent_pre_up).astype(jnp.bfloat16)
    target = matmul(parent_hidden, parent_down).astype(jnp.bfloat16)
    first_error, first_grad_gate, first_grad_up, first_grad_down = candidate_pass(inputs, target, first_gate, first_up, first_down)
    second_error, second_grad_gate, second_grad_up, second_grad_down = candidate_pass(inputs, target, second_gate, second_up, second_down)
    return (target, first_error, second_error, first_grad_gate, first_grad_up, first_grad_down, second_grad_gate, second_grad_up, second_grad_down)
```

```python
import functools

import jax
import jax.numpy as jnp
from jax import lax
from jax.experimental import pallas as pl
from jax.experimental.pallas import tpu as pltpu
from jax.sharding import PartitionSpec as P

MESH = pl.DeviceIdType.MESH
LANES = 128
PIECE = 1024
VMEM_BYTES = 48 * 1024 * 1024
F32 = jnp.float32
BF16 = jnp.bfloat16


def matmul(left, right):
    return jnp.dot(left, right, preferred_element_type=F32)


def inner_rows(left, right):
    return lax.dot_general(left, right, (((0,), (0,)), ((), ())), preferred_element_type=F32)


def outer_cols(left, right):
    return lax.dot_general(left, right, (((1,), (1,)), ((), ())), preferred_element_type=F32)


def cuts(width):
    units = width // LANES
    count = -(-width // PIECE)
    ranges, at = [], 0
    for i in range(count):
        size = (units // count + (i < units % count)) * LANES
        ranges.append((at, size))
        at += size
    return ranges


def remote(src, dst, send, recv, where):
    return pltpu.make_async_remote_copy(
        src_ref=src, dst_ref=dst, send_sem=send, recv_sem=recv,
        device_id=where, device_id_type=MESH,
    )


def exchange_kernel(grid_of, widths, forward, *refs):
    na, nb = grid_of
    count = len(widths)
    per_in, per_out = (2, 1) if forward else (1, 2)
    n_in = per_in * count
    refs = list(refs)
    partial = refs[:n_in]
    del refs[:n_in]
    if forward:
        gathered = refs[:count]
        share = refs[count:3 * count]
        del refs[:3 * count]
    else:
        share = refs[:2 * count]
        gathered = refs[2 * count:4 * count]
        del refs[:4 * count]
    got1, sum1, got2, s1, r1, s2, r2, s3, r3, s4, r4 = refs

    me = lax.axis_index("tok")
    hi, lo = me // nb, lax.rem(me, nb)
    hi_peers = [lax.rem(hi + d, na) for d in range(1, na)]
    lo_peers = [lax.rem(lo + d, nb) for d in range(1, nb)]

    jobs, at = [], 0
    for k, width in enumerate(widths):
        for start, size in cuts(width):
            jobs.append((k, start, size, at))
            at += size * per_in

    barrier = pltpu.get_barrier_semaphore()
    for peer in hi_peers:
        pl.semaphore_signal(barrier, inc=1, device_id={"tok": peer * nb + lo}, device_id_type=MESH)
    for peer in lo_peers:
        pl.semaphore_signal(barrier, inc=1, device_id={"tok": hi * nb + peer}, device_id_type=MESH)
    pl.semaphore_wait(barrier, na + nb - 2)

    pending = []
    first, second, third, fourth = {}, {}, {}, {}

    for j, (k, start, size, col) in enumerate(jobs):
        first[j] = []
        for d, peer in enumerate(lo_peers):
            for i in range(per_in):
                copy = remote(
                    partial[per_in * k + i].at[:, peer, :, pl.ds(start, size)],
                    got1.at[d, :, :, pl.ds(col + i * size, size)],
                    s1.at[j, d, i], r1.at[j, d, i], {"tok": hi * nb + peer},
                )
                copy.start()
                first[j].append(copy)
        pending += first[j]

    def add_low(j):
        k, start, size, col = jobs[j]
        for copy in first[j]:
            copy.wait_recv()
        for i in range(per_in):
            cols = pl.ds(col + i * size, size)
            total = partial[per_in * k + i][:, lo, :, pl.ds(start, size)].astype(F32)
            for d in range(nb - 1):
                total = total + got1[d, :, :, cols].astype(F32)
            sum1[:, :, cols] = total.astype(BF16)
        second[j] = []
        cols = pl.ds(col, size * per_in)
        for d, peer in enumerate(hi_peers):
            copy = remote(
                sum1.at[peer, :, cols], got2.at[d, :, cols], s2.at[j, d], r2.at[j, d],
                {"tok": peer * nb + lo},
            )
            copy.start()
            second[j].append(copy)
        pending.extend(second[j])

    def add_high(j):
        k, start, size, col = jobs[j]
        for copy in second[j]:
            copy.wait_recv()
        totals = []
        for i in range(per_in):
            cols = pl.ds(col + i * size, size)
            total = partial[per_in * k + i][hi, lo, :, pl.ds(start, size)].astype(F32)
            for d in range(nb - 1):
                total = total + got1[d, hi, :, cols].astype(F32)
            for d in range(na - 1):
                total = total + got2[d, :, cols].astype(F32)
            totals.append(total)
        window = pl.ds(start, size)
        if forward:
            gate, up = totals
            share[2 * k][:, window] = gate
            share[2 * k + 1][:, window] = up
            gathered[k][hi, lo, :, window] = (gate / (1.0 + jnp.exp(-gate)) * up).astype(BF16)
            outs = [gathered[k]]
        else:
            back = totals[0]
            gate = share[2 * k][:, window]
            up = share[2 * k + 1][:, window]
            s = 1.0 / (1.0 + jnp.exp(-gate))
            outs = [gathered[2 * k], gathered[2 * k + 1]]
            outs[0][hi, lo, :, window] = (back * up * s * (1.0 + gate * (1.0 - s))).astype(BF16)
            outs[1][hi, lo, :, window] = (back * gate * s).astype(BF16)
        third[j] = []
        for d, peer in enumerate(hi_peers):
            for i, out in enumerate(outs):
                here = out.at[hi, lo, :, window]
                copy = remote(
                    here, here, s3.at[j, d, i], r3.at[j, d, i], {"tok": peer * nb + lo}
                )
                copy.start()
                third[j].append(copy)
        pending.extend(third[j])

    def spread_low(j):
        k, start, size, col = jobs[j]
        for copy in third[j]:
            copy.wait_recv()
        outs = [gathered[per_out * k + i] for i in range(per_out)]
        fourth[j] = []
        for d, peer in enumerate(lo_peers):
            for i, out in enumerate(outs):
                here = out.at[:, lo, :, pl.ds(start, size)]
                copy = remote(
                    here, here, s4.at[j, d, i], r4.at[j, d, i], {"tok": hi * nb + peer}
                )
                copy.start()
                fourth[j].append(copy)
        pending.extend(fourth[j])

    total_jobs = len(jobs)
    for step in range(total_jobs + 2):
        if step < total_jobs:
            add_low(step)
        if 0 <= step - 1 < total_jobs:
            add_high(step - 1)
        if 0 <= step - 2 < total_jobs:
            spread_low(step - 2)
    for j in range(total_jobs):
        for copy in fourth[j]:
            copy.wait_recv()
    for copy in pending:
        copy.wait_send()


def exchange(arrays, shares, tok, forward, ident):
    na = 4 if tok % 4 == 0 else 1
    nb = tok // na
    per_in, per_out = (2, 1) if forward else (1, 2)
    count = len(arrays) // per_in
    tokens = arrays[0].shape[0]
    rows = tokens // tok
    real = [x.shape[1] for x in arrays]
    arrays = [jnp.pad(x, ((0, 0), (0, -x.shape[1] % LANES))) for x in arrays]
    widths = [arrays[per_in * k].shape[1] for k in range(count)]
    all_cols = per_in * sum(widths)
    n_jobs = sum(len(cuts(w)) for w in widths)
    gathered = [
        jax.ShapeDtypeStruct((na, nb, rows, w), BF16) for w in widths for _ in range(per_out)
    ]
    kept = [jax.ShapeDtypeStruct((rows, w), F32) for w in widths for _ in range(2)]
    lead = max(nb - 1, 1)
    dma = pltpu.SemaphoreType.DMA
    scratch = [
        pltpu.VMEM((lead, na, rows, all_cols), BF16),
        pltpu.VMEM((na, rows, all_cols), BF16),
        pltpu.VMEM((max(na - 1, 1), rows, all_cols), BF16),
        dma((n_jobs, lead, per_in)), dma((n_jobs, lead, per_in)),
        dma((n_jobs, max(na - 1, 1))), dma((n_jobs, max(na - 1, 1))),
        dma((n_jobs, max(na - 1, 1), per_out)), dma((n_jobs, max(na - 1, 1), per_out)),
        dma((n_jobs, lead, per_out)), dma((n_jobs, lead, per_out)),
    ]
    outs = gathered + kept if forward else gathered
    vmem = pl.BlockSpec(memory_space=pltpu.VMEM)
    operands = [x.reshape(na, nb, rows, x.shape[1]) for x in arrays] + list(shares)
    results = pl.pallas_call(
        functools.partial(exchange_kernel, (na, nb), widths, forward),
        out_shape=outs,
        in_specs=[vmem] * len(operands),
        out_specs=[vmem] * len(outs),
        scratch_shapes=scratch,
        compiler_params=pltpu.CompilerParams(
            collective_id=ident, has_side_effects=True, vmem_limit_bytes=VMEM_BYTES
        ),
        name="forward_exchange" if forward else "backward_exchange",
    )(*operands)
    full = [
        x.reshape(tokens, x.shape[-1])[:, : real[i * per_in // per_out]]
        for i, x in enumerate(results[: len(gathered)])
    ]
    return full, results[len(gathered):]


def hidden_group(sizes):
    ngrp, nwid = sizes
    total = ngrp * nwid
    me = lax.axis_index("grp") * nwid + lax.axis_index("wid")
    peers = [lax.rem(me + d, total) for d in range(1, total)]
    places = [{"grp": p // nwid, "wid": lax.rem(p, nwid)} for p in peers]
    barrier = pltpu.get_barrier_semaphore()
    for place in places:
        pl.semaphore_signal(barrier, inc=1, device_id=place, device_id_type=MESH)
    pl.semaphore_wait(barrier, total - 1)
    return me, peers, places


def gather_kernel(sizes, x_ref, out_ref, own, send, recv):
    me, peers, places = hidden_group(sizes)
    copies = []
    for d, place in enumerate(places):
        copy = remote(x_ref, out_ref.at[me], send.at[d], recv.at[d], place)
        copy.start()
        copies.append(copy)
    local = pltpu.make_async_copy(x_ref, out_ref.at[me], own)
    local.start()
    local.wait()
    for copy in copies:
        copy.wait()


def gather_rows(x, sizes):
    total = sizes[0] * sizes[1]
    vmem = pl.BlockSpec(memory_space=pltpu.VMEM)
    dma = pltpu.SemaphoreType.DMA
    out = pl.pallas_call(
        functools.partial(gather_kernel, sizes),
        out_shape=jax.ShapeDtypeStruct((total,) + x.shape, x.dtype),
        in_specs=[vmem],
        out_specs=vmem,
        scratch_shapes=[dma, dma((total - 1,)), dma((total - 1,))],
        compiler_params=pltpu.CompilerParams(collective_id=0, has_side_effects=True),
        name="gather_rows",
    )(x)
    return out.reshape(total * x.shape[0], x.shape[1])


def errors_kernel(
    sizes, t_ref, a_ref, b_ref, target, a_err, b_err, a_all, b_all, got, s1, r1, s2, r2
):
    me, peers, places = hidden_group(sizes)
    sources = (t_ref, a_ref, b_ref)
    copies = []
    for i, source in enumerate(sources):
        for d, (peer, place) in enumerate(zip(peers, places)):
            copy = remote(source.at[peer], got.at[d, i], s1.at[d, i], r1.at[d, i], place)
            copy.start()
            copies.append(copy)
    for copy in copies:
        copy.wait_recv()
    totals = []
    for i, source in enumerate(sources):
        total = source[me].astype(F32)
        for d in range(len(peers)):
            total = total + got[d, i].astype(F32)
        totals.append(total)
    goal = totals[0].astype(BF16)
    target[...] = goal
    goal = goal.astype(F32)
    sends = []
    for i, (total, own, full) in enumerate(
        ((totals[1], a_err, a_all), (totals[2], b_err, b_all))
    ):
        value = (total - goal).astype(BF16)
        own[...] = value
        full[me] = value
        for d, place in enumerate(places):
            copy = remote(full.at[me], full.at[me], s2.at[d, i], r2.at[d, i], place)
            copy.start()
            sends.append(copy)
    for copy in sends:
        copy.wait_recv()
    for copy in copies + sends:
        copy.wait_send()


def errors(parts, sizes):
    total = sizes[0] * sizes[1]
    tokens, features = parts[0].shape
    rows = tokens // total
    vmem = pl.BlockSpec(memory_space=pltpu.VMEM)
    dma = pltpu.SemaphoreType.DMA
    own = jax.ShapeDtypeStruct((rows, features), BF16)
    full = jax.ShapeDtypeStruct((total, rows, features), BF16)
    target, a_err, b_err, a_all, b_all = pl.pallas_call(
        functools.partial(errors_kernel, sizes),
        out_shape=[own, own, own, full, full],
        in_specs=[vmem] * 3,
        out_specs=[vmem] * 5,
        scratch_shapes=[
            pltpu.VMEM((total - 1, 3, rows, features), BF16),
            dma((total - 1, 3)), dma((total - 1, 3)), dma((total - 1, 2)), dma((total - 1, 2)),
        ],
        compiler_params=pltpu.CompilerParams(
            collective_id=1, has_side_effects=True, vmem_limit_bytes=VMEM_BYTES
        ),
        name="errors",
    )(*[x.reshape(total, rows, features) for x in parts])
    return target, a_err, b_err, a_all.reshape(tokens, -1), b_all.reshape(tokens, -1)


def outer_kernel(left, gate, up, gate_out, up_out):
    gate_out[...] = matmul(left[...], gate[...]).astype(BF16)
    up_out[...] = matmul(left[...], up[...]).astype(BF16)


def weight_grads(columns_t, gate, up):
    features, tokens = columns_t.shape
    width = gate.shape[1]
    tile = next((t for t in (256, LANES) if width % t == 0), width)
    block = pl.BlockSpec((tokens, tile), lambda i: (0, i))
    out_block = pl.BlockSpec((features, tile), lambda i: (0, i))
    out = jax.ShapeDtypeStruct((features, width), BF16)
    return pl.pallas_call(
        outer_kernel,
        grid=(width // tile,),
        out_shape=[out, out],
        in_specs=[pl.BlockSpec((features, tokens), lambda i: (0, 0)), block, block],
        out_specs=[out_block, out_block],
        compiler_params=pltpu.CompilerParams(vmem_limit_bytes=VMEM_BYTES),
        cost_estimate=pl.CostEstimate(
            flops=4 * features * tokens * width,
            bytes_accessed=4 * (features + tokens) * width,
            transcendentals=0,
        ),
        name="weight_grads",
    )(columns_t, gate, up)


def body(
    tok, sizes, inputs, parent_gate, parent_up, parent_down, first_gate, first_up, first_down,
    second_gate, second_up, second_down,
):
    columns = gather_rows(inputs, sizes)
    weights = (parent_gate, parent_up, first_gate, first_up, second_gate, second_up)
    partials = [matmul(columns, w).astype(BF16) for w in weights]
    (parent_hidden, first_hidden, second_hidden), kept = exchange(partials, (), tok, True, 2)
    outs = [
        matmul(parent_hidden, parent_down).astype(BF16),
        matmul(first_hidden, first_down).astype(BF16),
        matmul(second_hidden, second_down).astype(BF16),
    ]
    target, first_error, second_error, first_all, second_all = errors(outs, sizes)
    backs = [
        outer_cols(first_all, first_down).astype(BF16),
        outer_cols(second_all, second_down).astype(BF16),
    ]
    grads, _ = exchange(backs, kept[2:], tok, False, 3)
    first_grad_down = inner_rows(first_hidden, first_all).astype(BF16)
    second_grad_down = inner_rows(second_hidden, second_all).astype(BF16)
    columns_t = columns.T
    first_grad_gate, first_grad_up = weight_grads(columns_t, grads[0], grads[1])
    second_grad_gate, second_grad_up = weight_grads(columns_t, grads[2], grads[3])
    return (
        target, first_error, second_error,
        first_grad_gate, first_grad_up, first_grad_down,
        second_grad_gate, second_grad_up, second_grad_down,
    )


def solution(mesh):
    tok = mesh.shape["tok"]
    sizes = (mesh.shape["grp"], mesh.shape["wid"])
    rows = P(("grp", "wid"), "tok")
    cols = P("tok", ("grp", "wid"))
    return jax.shard_map(
        functools.partial(body, tok, sizes),
        mesh=mesh,
        in_specs=(rows, cols, cols, rows, cols, cols, rows, cols, cols, rows),
        out_specs=(rows, rows, rows, cols, cols, rows, cols, cols, rows),
        check_vma=False,
    )
```

```python
import functools

import jax
import jax.numpy as jnp
from jax import lax
from jax.experimental import pallas as pl
from jax.experimental.pallas import tpu as pltpu
from jax.sharding import PartitionSpec as P

MESH = pl.DeviceIdType.MESH
LANES = 128
PIECE = 1024
MIB = 1024 * 1024
SLOTS = 4
F32 = jnp.float32
BF16 = jnp.bfloat16


def matmul(left, right):
    return jnp.dot(left, right, preferred_element_type=F32)


def inner_rows(left, right):
    return lax.dot_general(left, right, (((0,), (0,)), ((), ())), preferred_element_type=F32)


def outer_cols(left, right):
    return lax.dot_general(left, right, (((1,), (1,)), ((), ())), preferred_element_type=F32)


def cuts(width):
    units = width // LANES
    count = -(-width // PIECE)
    ranges, at = [], 0
    for i in range(count):
        size = (units // count + (i < units % count)) * LANES
        ranges.append((at, size))
        at += size
    return ranges


def remote(src, dst, send, recv, where):
    return pltpu.make_async_remote_copy(
        src_ref=src, dst_ref=dst, send_sem=send, recv_sem=recv,
        device_id=where, device_id_type=MESH,
    )


def exchange_kernel(grid_of, widths, forward, *refs):
    na, nb = grid_of
    count = len(widths)
    per_in, per_out = (2, 1) if forward else (1, 2)
    refs = list(refs)
    if forward:
        left, weights = refs[0], refs[1:3]
        partial = [refs[-4], refs[-3]] + refs[3:2 * count + 1]
        held, loaded = refs[-2], refs[-1]
        del refs[:2 * count + 1]
        del refs[-4:]
    else:
        partial = refs[:count]
        del refs[:count]
    if forward:
        gathered = refs[:count]
        share = refs[count:3 * count]
        del refs[:3 * count]
    else:
        share = refs[:2 * count]
        gathered = refs[2 * count:4 * count]
        del refs[:4 * count]
    got1, sum1, got2, s1, r1, s2, r2, s3, r3, s4, r4 = refs

    me = lax.axis_index("tok")
    hi, lo = me // nb, lax.rem(me, nb)
    hi_peers = [lax.rem(hi + d, na) for d in range(1, na)]
    lo_peers = [lax.rem(lo + d, nb) for d in range(1, nb)]

    jobs, at = [], 0
    order = list(range(1, count)) + [0] if forward else list(range(count))
    for k in order:
        for start, size in cuts(widths[k]):
            jobs.append((k, start, size, at))
            at += size * per_in
    made = [j for j, job in enumerate(jobs) if forward and job[0] == 0]

    def load(n):
        k, start, size, col = jobs[made[n]]
        return [
            pltpu.make_async_copy(
                weights[i].at[:, pl.ds(start, size)],
                held.at[n % SLOTS, i, :, pl.ds(0, size)],
                loaded.at[n % SLOTS, i],
            )
            for i in range(2)
        ]

    for n in range(min(SLOTS, len(made))):
        for copy in load(n):
            copy.start()

    barrier = pltpu.get_barrier_semaphore()
    for peer in hi_peers:
        pl.semaphore_signal(barrier, inc=1, device_id={"tok": peer * nb + lo}, device_id_type=MESH)
    for peer in lo_peers:
        pl.semaphore_signal(barrier, inc=1, device_id={"tok": hi * nb + peer}, device_id_type=MESH)
    pl.semaphore_wait(barrier, na + nb - 2)

    pending = []
    first, second, third, fourth = {}, {}, {}, {}

    def send_low(j):
        k, start, size, col = jobs[j]
        if j in made:
            n = made.index(j)
            for i, copy in enumerate(load(n)):
                copy.wait()
                product = matmul(left[...], held[n % SLOTS, i, :, pl.ds(0, size)]).astype(BF16)
                partial[i][:, :, :, pl.ds(start, size)] = product.reshape(
                    na, nb, left.shape[0] // (na * nb), size
                )
            if n + SLOTS < len(made):
                for copy in load(n + SLOTS):
                    copy.start()
        first[j] = []
        for d, peer in enumerate(lo_peers):
            for i in range(per_in):
                copy = remote(
                    partial[per_in * k + i].at[:, peer, :, pl.ds(start, size)],
                    got1.at[d, :, :, pl.ds(col + i * size, size)],
                    s1.at[j, d, i], r1.at[j, d, i], {"tok": hi * nb + peer},
                )
                copy.start()
                first[j].append(copy)
        pending.extend(first[j])

    def add_low(j):
        k, start, size, col = jobs[j]
        for copy in first[j]:
            copy.wait_recv()
        for i in range(per_in):
            cols = pl.ds(col + i * size, size)
            total = partial[per_in * k + i][:, lo, :, pl.ds(start, size)].astype(F32)
            for d in range(nb - 1):
                total = total + got1[d, :, :, cols].astype(F32)
            sum1[:, :, cols] = total.astype(BF16)
        second[j] = []
        cols = pl.ds(col, size * per_in)
        for d, peer in enumerate(hi_peers):
            copy = remote(
                sum1.at[peer, :, cols], got2.at[d, :, cols], s2.at[j, d], r2.at[j, d],
                {"tok": peer * nb + lo},
            )
            copy.start()
            second[j].append(copy)
        pending.extend(second[j])

    def add_high(j):
        k, start, size, col = jobs[j]
        for copy in second[j]:
            copy.wait_recv()
        totals = []
        for i in range(per_in):
            cols = pl.ds(col + i * size, size)
            total = partial[per_in * k + i][hi, lo, :, pl.ds(start, size)].astype(F32)
            for d in range(nb - 1):
                total = total + got1[d, hi, :, cols].astype(F32)
            for d in range(na - 1):
                total = total + got2[d, :, cols].astype(F32)
            totals.append(total)
        window = pl.ds(start, size)
        if forward:
            gate, up = totals
            share[2 * k][:, window] = gate
            share[2 * k + 1][:, window] = up
            gathered[k][hi, lo, :, window] = (gate / (1.0 + jnp.exp(-gate)) * up).astype(BF16)
            outs = [gathered[k]]
        else:
            back = totals[0]
            gate = share[2 * k][:, window]
            up = share[2 * k + 1][:, window]
            s = 1.0 / (1.0 + jnp.exp(-gate))
            outs = [gathered[2 * k], gathered[2 * k + 1]]
            outs[0][hi, lo, :, window] = (back * up * s * (1.0 + gate * (1.0 - s))).astype(BF16)
            outs[1][hi, lo, :, window] = (back * gate * s).astype(BF16)
        third[j] = []
        for d, peer in enumerate(hi_peers):
            for i, out in enumerate(outs):
                here = out.at[hi, lo, :, window]
                copy = remote(
                    here, here, s3.at[j, d, i], r3.at[j, d, i], {"tok": peer * nb + lo}
                )
                copy.start()
                third[j].append(copy)
        pending.extend(third[j])

    def spread_low(j):
        k, start, size, col = jobs[j]
        for copy in third[j]:
            copy.wait_recv()
        outs = [gathered[per_out * k + i] for i in range(per_out)]
        fourth[j] = []
        for d, peer in enumerate(lo_peers):
            for i, out in enumerate(outs):
                here = out.at[:, lo, :, pl.ds(start, size)]
                copy = remote(
                    here, here, s4.at[j, d, i], r4.at[j, d, i], {"tok": hi * nb + peer}
                )
                copy.start()
                fourth[j].append(copy)
        pending.extend(fourth[j])

    total_jobs = len(jobs)
    ahead = total_jobs - len(made) + 1 if made else total_jobs
    for j in range(min(ahead, total_jobs)):
        send_low(j)
    for step in range(total_jobs + 2):
        if step + ahead < total_jobs:
            send_low(step + ahead)
        if step < total_jobs:
            add_low(step)
        if 0 <= step - 1 < total_jobs:
            add_high(step - 1)
        if 0 <= step - 2 < total_jobs:
            spread_low(step - 2)
    for j in range(total_jobs):
        for copy in fourth[j]:
            copy.wait_recv()
    for copy in pending:
        copy.wait_send()


def padded(x):
    return jnp.pad(x, ((0, 0), (0, -x.shape[1] % LANES)))


def exchange(arrays, shares, tok, forward, ident, product=()):
    na = 4 if tok % 4 == 0 else 1
    nb = tok // na
    per_in, per_out = (2, 1) if forward else (1, 2)
    tokens = arrays[0].shape[0]
    rows = tokens // tok
    real = [x.shape[1] for x in tuple(product[1:]) + tuple(arrays)]
    product = list(product[:1]) + [padded(x) for x in product[1:]]
    arrays = [padded(x) for x in arrays]
    all_widths = [x.shape[1] for x in product[1:] + arrays]
    widths = all_widths[::per_in]
    count = len(widths)
    all_cols = per_in * sum(widths)
    n_jobs = sum(len(cuts(w)) for w in widths)
    gathered = [
        jax.ShapeDtypeStruct((na, nb, rows, w), BF16) for w in widths for _ in range(per_out)
    ]
    kept = [jax.ShapeDtypeStruct((rows, w), F32) for w in widths for _ in range(2)]
    lead = max(nb - 1, 1)
    dma = pltpu.SemaphoreType.DMA
    scratch = [
        pltpu.VMEM((lead, na, rows, all_cols), BF16),
        pltpu.VMEM((na, rows, all_cols), BF16),
        pltpu.VMEM((max(na - 1, 1), rows, all_cols), BF16),
        dma((n_jobs, lead, per_in)), dma((n_jobs, lead, per_in)),
        dma((n_jobs, max(na - 1, 1))), dma((n_jobs, max(na - 1, 1))),
        dma((n_jobs, max(na - 1, 1), per_out)), dma((n_jobs, max(na - 1, 1), per_out)),
        dma((n_jobs, lead, per_out)), dma((n_jobs, lead, per_out)),
    ]
    outs = gathered + kept if forward else gathered
    vmem = pl.BlockSpec(memory_space=pltpu.VMEM)
    in_specs = [vmem] * (len(arrays) + len(shares))
    if forward:
        piece = max(size for _, size in cuts(widths[0]))
        scratch += [pltpu.VMEM((na, nb, rows, widths[0]), BF16)] * 2
        scratch += [
            pltpu.VMEM((SLOTS, 2, product[0].shape[1], piece), BF16), dma((SLOTS, 2)),
        ]
        in_specs = [vmem] + [pl.BlockSpec(memory_space=pl.ANY)] * 2 + in_specs
    operands = product + [x.reshape(na, nb, rows, x.shape[1]) for x in arrays] + list(shares)
    results = pl.pallas_call(
        functools.partial(exchange_kernel, (na, nb), widths, forward),
        out_shape=outs,
        in_specs=in_specs,
        out_specs=[vmem] * len(outs),
        scratch_shapes=scratch,
        compiler_params=pltpu.CompilerParams(
            collective_id=ident, has_side_effects=True,
            vmem_limit_bytes=(36 if forward else 10) * MIB,
        ),
        name="forward_exchange" if forward else "backward_exchange",
    )(*operands)
    full = [
        x.reshape(tokens, x.shape[-1])[:, : real[i * per_in // per_out]]
        for i, x in enumerate(results[: len(gathered)])
    ]
    return full, results[len(gathered):]


def hidden_group(sizes):
    ngrp, nwid = sizes
    total = ngrp * nwid
    me = lax.axis_index("grp") * nwid + lax.axis_index("wid")
    peers = [lax.rem(me + d, total) for d in range(1, total)]
    places = [{"grp": p // nwid, "wid": lax.rem(p, nwid)} for p in peers]
    barrier = pltpu.get_barrier_semaphore()
    for place in places:
        pl.semaphore_signal(barrier, inc=1, device_id=place, device_id_type=MESH)
    pl.semaphore_wait(barrier, total - 1)
    return me, peers, places


def gather_kernel(sizes, x_ref, out_ref, own, send, recv):
    me, peers, places = hidden_group(sizes)
    copies = []
    for d, place in enumerate(places):
        copy = remote(x_ref, out_ref.at[me], send.at[d], recv.at[d], place)
        copy.start()
        copies.append(copy)
    local = pltpu.make_async_copy(x_ref, out_ref.at[me], own)
    local.start()
    local.wait()
    for copy in copies:
        copy.wait()


def gather_rows(x, sizes):
    total = sizes[0] * sizes[1]
    vmem = pl.BlockSpec(memory_space=pltpu.VMEM)
    dma = pltpu.SemaphoreType.DMA
    out = pl.pallas_call(
        functools.partial(gather_kernel, sizes),
        out_shape=jax.ShapeDtypeStruct((total,) + x.shape, x.dtype),
        in_specs=[vmem],
        out_specs=vmem,
        scratch_shapes=[dma, dma((total - 1,)), dma((total - 1,))],
        compiler_params=pltpu.CompilerParams(
            collective_id=0, has_side_effects=True, vmem_limit_bytes=4 * MIB
        ),
        name="gather_rows",
    )(x)
    return out.reshape(total * x.shape[0], x.shape[1])


def down_step(features):
    return 256 if features % 256 == 0 else features


def errors_kernel(
    sizes, hidden, down, a_ref, b_ref, target, a_err, b_err, a_all, b_all, t_ref, got,
    s1, r1, s2, r2, s3, r3,
):
    me, peers, places = hidden_group(sizes)
    sources = (t_ref, a_ref, b_ref)
    copies = []
    for i in (1, 2):
        for d, (peer, place) in enumerate(zip(peers, places)):
            copy = remote(sources[i].at[peer], got.at[d, i], s1.at[d, i], r1.at[d, i], place)
            copy.start()
            copies.append(copy)
    total, rows, features = t_ref.shape
    step = down_step(features)
    for c in range(features // step):
        cols = pl.ds(c * step, step)
        part = matmul(hidden[...], down[:, cols])
        t_ref[:, :, cols] = part.astype(BF16).reshape(total, rows, step)
        for d, (peer, place) in enumerate(zip(peers, places)):
            copy = remote(
                t_ref.at[peer, :, cols], got.at[d, 0, :, cols], s3.at[d, c], r3.at[d, c], place
            )
            copy.start()
            copies.append(copy)
    for copy in copies:
        copy.wait_recv()
    totals = []
    for i, source in enumerate(sources):
        total = source[me].astype(F32)
        for d in range(len(peers)):
            total = total + got[d, i].astype(F32)
        totals.append(total)
    goal = totals[0].astype(BF16)
    target[...] = goal
    goal = goal.astype(F32)
    sends = []
    for i, (total, own, full) in enumerate(
        ((totals[1], a_err, a_all), (totals[2], b_err, b_all))
    ):
        value = (total - goal).astype(BF16)
        own[...] = value
        full[me] = value
        for d, place in enumerate(places):
            copy = remote(full.at[me], full.at[me], s2.at[d, i], r2.at[d, i], place)
            copy.start()
            sends.append(copy)
    for copy in sends:
        copy.wait_recv()
    for copy in copies + sends:
        copy.wait_send()


def errors(hidden, down, parts, sizes):
    total = sizes[0] * sizes[1]
    tokens, features = parts[0].shape
    pieces = features // down_step(features)
    rows = tokens // total
    vmem = pl.BlockSpec(memory_space=pltpu.VMEM)
    dma = pltpu.SemaphoreType.DMA
    own = jax.ShapeDtypeStruct((rows, features), BF16)
    full = jax.ShapeDtypeStruct((total, rows, features), BF16)
    target, a_err, b_err, a_all, b_all = pl.pallas_call(
        functools.partial(errors_kernel, sizes),
        out_shape=[own, own, own, full, full],
        in_specs=[vmem] * 4,
        out_specs=[vmem] * 5,
        scratch_shapes=[
            pltpu.VMEM((total, rows, features), BF16),
            pltpu.VMEM((total - 1, 3, rows, features), BF16),
            dma((total - 1, 3)), dma((total - 1, 3)), dma((total - 1, 2)), dma((total - 1, 2)),
            dma((total - 1, pieces)), dma((total - 1, pieces)),
        ],
        compiler_params=pltpu.CompilerParams(
            collective_id=1, has_side_effects=True, vmem_limit_bytes=24 * MIB
        ),
        name="errors",
    )(hidden, down, *[x.reshape(total, rows, features) for x in parts])
    return target, a_err, b_err, a_all.reshape(tokens, -1), b_all.reshape(tokens, -1)


def outer_kernel(columns, *refs):
    half = len(refs) // 2
    left = columns[...].T
    for grad, out in zip(refs[:half], refs[half:]):
        out[...] = matmul(left, grad[...]).astype(BF16)


def weight_grads(columns, grads):
    tokens, features = columns.shape
    tile = LANES
    out_bytes = 2 * features * sum(g.shape[1] for g in grads)
    return pl.pallas_call(
        outer_kernel,
        grid=(features // tile,),
        out_shape=[jax.ShapeDtypeStruct((features, g.shape[1]), BF16) for g in grads],
        in_specs=[pl.BlockSpec((tokens, tile), lambda i: (0, i))]
        + [pl.BlockSpec(memory_space=pltpu.VMEM)] * len(grads),
        out_specs=[pl.BlockSpec((tile, g.shape[1]), lambda i: (i, 0)) for g in grads],
        compiler_params=pltpu.CompilerParams(vmem_limit_bytes=16 * MIB),
        cost_estimate=pl.CostEstimate(
            flops=tokens * out_bytes, bytes_accessed=out_bytes, transcendentals=0
        ),
        name="weight_grads",
    )(columns, *grads)


def body(
    tok, sizes, inputs, parent_gate, parent_up, parent_down, first_gate, first_up, first_down,
    second_gate, second_up, second_down,
):
    columns = gather_rows(inputs, sizes)
    weights = (first_gate, first_up, second_gate, second_up)
    partials = [matmul(columns, w).astype(BF16) for w in weights]
    (parent_hidden, first_hidden, second_hidden), kept = exchange(
        partials, (), tok, True, 2, (columns, parent_gate, parent_up)
    )
    outs = [
        matmul(first_hidden, first_down).astype(BF16),
        matmul(second_hidden, second_down).astype(BF16),
    ]
    target, first_error, second_error, first_all, second_all = errors(
        parent_hidden, parent_down, outs, sizes
    )
    backs = [
        outer_cols(first_all, first_down).astype(BF16),
        outer_cols(second_all, second_down).astype(BF16),
    ]
    grads, _ = exchange(backs, kept[2:], tok, False, 3)
    first_grad_down = inner_rows(first_hidden, first_all).astype(BF16)
    second_grad_down = inner_rows(second_hidden, second_all).astype(BF16)
    first_grad_gate, first_grad_up, second_grad_gate, second_grad_up = weight_grads(
        columns, grads
    )
    return (
        target, first_error, second_error,
        first_grad_gate, first_grad_up, first_grad_down,
        second_grad_gate, second_grad_up, second_grad_down,
    )


def solution(mesh):
    tok = mesh.shape["tok"]
    sizes = (mesh.shape["grp"], mesh.shape["wid"])
    rows = P(("grp", "wid"), "tok")
    cols = P("tok", ("grp", "wid"))
    return jax.shard_map(
        functools.partial(body, tok, sizes),
        mesh=mesh,
        in_specs=(rows, cols, cols, rows, cols, cols, rows, cols, cols, rows),
        out_specs=(rows, rows, rows, cols, cols, rows, cols, cols, rows),
        check_vma=False,
    )
```
